256 devices in a mesh: rep: 16 (over z_lo, x), tp: 16 (over y, z_hi, core).
Axes of the slice: x: 4, y: 4, z: 8 (z_hi: 2, z_lo: 4; z = z_hi * 4 + z_lo), core: 2. Of those that a mesh axis runs over, the one named last changes fastest.
Arguments:
- queries: bfloat16 [16, 512, 4096], P('rep', None, 'tp'), may hold values from -120 to 120
- keys: bfloat16 [16, 512, 4096], P('rep', None, 'tp'), may hold values from -6 to 6
- values: bfloat16 [16, 512, 4096], P('rep', None, 'tp'), may hold values from -6 to 6
- out_weight: bfloat16 [16, 4096, 7168], P('rep', 'tp'), may hold values from -0.09375 to 0.09375
- cotangent: bfloat16 [16, 512, 7168], P('rep', 'tp'), may hold values from -6 to 6
- local_params: bfloat16 [16, 2, 128, 7168], P('rep', None, 'tp'), may hold values from -6 to 6
- global_params: float32 [2, 128, 7168], P(None, 'tp'), may hold values from -6 to 6
- momentum: float32 [2, 128, 7168], P(None, 'tp'), may hold values from -3 to 3
- frag_index: int32 [1], replicated, may hold values from 0 to 1
Outputs:
- branch_out: bfloat16 [16, 512, 7168], P('rep', 'tp')
- weight_grad: bfloat16 [16, 4096, 7168], P('rep', 'tp')
- query_grad: bfloat16 [16, 512, 4096], P('rep', None, 'tp')
- key_grad: bfloat16 [16, 512, 4096], P('rep', None, 'tp')
- value_grad: bfloat16 [16, 512, 4096], P('rep', None, 'tp')
- new_global: float32 [128, 7168], P('tp')
- new_momentum: float32 [128, 7168], P('tp')
The draws below stay inside these ranges and needn't reach their ends.
All inputs are finite; a program needn't handle non-finite values.
Results may differ from the reference program's by a relative error of at most 0.017.
Values may be sent and summed in bfloat16 or wider, within the bound.
No kernel may reach another device: no remote copies, remote signals or barrier semaphores. Data moves between devices by JAX's collectives and lax.ppermute only.
A program may use at most 128 MiB of HBM per device.

```python
import jax
import jax.numpy as jnp
from jax import lax

D = 7168
HD = 128
HEADS_DEV = 2
LEN = 512
SEQS = 1
FRAGS = 2
HEADS = 32
TOKENS = 512
FRAG_ROWS = 128
N_REP = 16
N_TP = 16


def query_key_pair(key):
    shape = (N_REP, TOKENS, HEADS * HD)
    base_query = jnp.clip(jax.random.normal(jax.random.fold_in(key, 11), shape, jnp.float32), -6.0, 6.0)
    base_key = jnp.clip(jax.random.normal(jax.random.fold_in(key, 12), shape, jnp.float32), -6.0, 6.0)
    return (base_query, base_key)


def draw_queries(key, part):
    base_query, base_key = query_key_pair(key)
    return base_query.astype(jnp.bfloat16)


def draw_keys(key, part):
    base_query, base_key = query_key_pair(key)
    return base_key.astype(jnp.bfloat16)


def shard_levels(stream_key, extent, split, low, top_value):
    loudness = 1.0
    for dim, blocks in split:
        draws = jax.random.uniform(jax.random.fold_in(jax.random.fold_in(stream_key, 6), dim), (blocks,), jnp.float32, low / len(split), top_value / len(split))
        loudness = loudness * jnp.repeat(jnp.exp(draws), extent[dim] // blocks).reshape((-1,) + (1,) * (len(extent) - 1 - dim))
    return loudness


def gaussian(own_key, shape, spread, most, pieces=(), dtype=jnp.bfloat16):
    entries = jax.random.normal(own_key, shape, jnp.float32) * spread
    if len(pieces) > 0:
        entries = shard_levels(own_key, shape, pieces, -0.22, 0.18) * entries
    return jnp.clip(entries, min=-most, max=most).astype(dtype)


def setup_inputs(seed: int = 0) -> dict:
    key_list = jax.random.split(jax.random.key(seed), 10)
    queries = draw_queries(jax.random.fold_in(key_list[9], 71), 0)
    keys = draw_keys(jax.random.fold_in(key_list[9], 71), 0)
    values = gaussian(key_list[2], (N_REP, TOKENS, HEADS * HD), 1.0, 6.0, ((0, 16), (2, 16)))
    out_weight = gaussian(key_list[3], (N_REP, HEADS * HD, D), (HEADS * HD) ** -0.5, 0.09375, ((0, 16), (1, 16)))
    cotangent = gaussian(key_list[4], (N_REP, TOKENS, D), 1.0, 6.0, ((0, 16), (1, 16)))
    local_params = gaussian(key_list[5], (N_REP, FRAGS, FRAG_ROWS, D), 1.0, 6.0, ((0, 16), (2, 16)))
    global_params = gaussian(key_list[6], (FRAGS, FRAG_ROWS, D), 1.0, 6.0, ((1, 16),), jnp.float32)
    momentum = gaussian(key_list[7], (FRAGS, FRAG_ROWS, D), 0.5, 3.0, ((1, 16),), jnp.float32)
    frag_index = jax.random.randint(key_list[8], (1,), 0, FRAGS).astype(jnp.int32)
    return dict(queries=queries, keys=keys, values=values, out_weight=out_weight, cotangent=cotangent, local_params=local_params, global_params=global_params, momentum=momentum, frag_index=frag_index)


outer_momentum = 0.9
outer_rate = 0.7


def split_heads(array):
    return array.reshape(SEQS, LEN, HEADS, HD).astype(jnp.float32)


def one_replica(inputs):
    queries, keys, values, out_weight, cotangent = inputs
    scale = HD ** -0.5
    query_heads = split_heads(queries)
    key_heads = split_heads(keys)
    value_heads = split_heads(values)
    scores = jnp.einsum("slhd,smhd->shlm", query_heads, key_heads) * scale
    causal = jnp.arange(LEN)[:, None] >= jnp.arange(LEN)[None, :]
    scores = jnp.where(causal[None, None], scores, -1e30)
    top = jnp.max(scores, axis=-1, keepdims=True)
    weights = jnp.exp(scores - top)
    probs = weights / jnp.sum(weights, axis=-1, keepdims=True)
    probs_half = probs.astype(jnp.bfloat16)
    context = jnp.einsum("shlm,smhd->slhd", probs_half.astype(jnp.float32), value_heads)
    context = context.astype(jnp.bfloat16).reshape(TOKENS, HEADS * HD)
    group_cols = HEADS_DEV * HD
    context_groups = context.reshape(TOKENS, N_TP, group_cols).transpose(1, 0, 2)
    weight_groups = out_weight.reshape(N_TP, group_cols, D)

    def add_group(summed, pair):
        partial_term = jnp.dot(pair[0], pair[1], preferred_element_type=jnp.float32).astype(jnp.bfloat16)
        partial_term = lax.optimization_barrier(partial_term)
        return summed + partial_term.astype(jnp.float32), None

    summed, unused = lax.scan(add_group, jnp.zeros((TOKENS, D), jnp.float32), (context_groups, weight_groups))
    branch_out = summed.astype(jnp.bfloat16)
    weight_grad = jnp.dot(context.T, cotangent, preferred_element_type=jnp.float32).astype(jnp.bfloat16)
    context_grad = jnp.dot(cotangent, out_weight.T, preferred_element_type=jnp.float32).astype(jnp.bfloat16)
    context_heads = split_heads(context_grad)
    probs_grad = jnp.einsum("slhd,smhd->shlm", context_heads, value_heads)
    inner = jnp.sum(probs * probs_grad, axis=-1, keepdims=True)
    score_grad = (probs * (probs_grad - inner) * scale).astype(jnp.bfloat16).astype(jnp.float32)
    query_grad = jnp.einsum("shlm,smhd->slhd", score_grad, key_heads)
    key_grad = jnp.einsum("shlm,slhd->smhd", score_grad, query_heads)
    value_grad = jnp.einsum("shlm,slhd->smhd", probs_half.astype(jnp.float32), context_heads)
    shaped = [g.astype(jnp.bfloat16).reshape(TOKENS, HEADS * HD) for g in (query_grad, key_grad, value_grad)]
    return branch_out, weight_grad, shaped[0], shaped[1], shaped[2]


def reference(queries, keys, values, out_weight, cotangent, local_params, global_params, momentum, frag_index):
    results = lax.map(one_replica, (queries, keys, values, out_weight, cotangent))
    chosen = frag_index[0].astype(jnp.int32)
    local_sel = lax.dynamic_index_in_dim(local_params, chosen, 1, keepdims=False).astype(jnp.float32)
    average = jnp.sum(local_sel, axis=0) / N_REP
    outer_old = lax.dynamic_index_in_dim(global_params, chosen, 0, keepdims=False)
    moment_old = lax.dynamic_index_in_dim(momentum, chosen, 0, keepdims=False)
    pseudo_grad = outer_old - average
    new_momentum = outer_momentum * moment_old + pseudo_grad
    new_global = outer_old - outer_rate * (outer_momentum * new_momentum + pseudo_grad)
    return results[0], results[1], results[2], results[3], results[4], new_global, new_momentum
```

```python
import functools

import jax
import jax.numpy as jnp
from jax import lax
from jax.experimental import pallas as pl
from jax.experimental.pallas import tpu as pltpu
from jax.sharding import PartitionSpec as P

HD = 128
ROWS = 128
N_Y = 4
F32 = jnp.float32
BF16 = jnp.bfloat16

outer_momentum = 0.9
outer_rate = 0.7
ANY = pl.ANY
SMEM = pltpu.SMEM


def tp_index(y, z, c):
    return (y % N_Y) * 4 + z * 2 + c


def tp_moves(move):
    return [
        (tp_index(y, z, c), tp_index(*move(y, z, c)))
        for y in range(N_Y)
        for z in range(2)
        for c in range(2)
    ]


AHEAD = tp_moves(lambda y, z, c: (y + 1 - 2 * c, z, c))
BACK = tp_moves(lambda y, z, c: (y - 1 + 2 * c, z, c))
ACROSS = tp_moves(lambda y, z, c: (y, 1 - z, c))
OTHER_CORE = tp_moves(lambda y, z, c: (y, z, 1 - c))
REP_STEPS = [[(r, r ^ bit) for r in range(16)] for bit in (1, 2, 4, 8)]


def send(value, moves, axis="tp"):
    return lax.ppermute(value, axis, moves)


def forward_kernel(core_ref, q_ref, k_ref, v_ref, ctx_ref, keep_ref, give_ref, probs_ref):
    scale = HD ** (-0.5)
    core = core_ref[0]
    tokens = q_ref.shape[0]
    for i in range(tokens // ROWS):
        n = ROWS * (i + 1)
        mine = pl.ds(i * ROWS, ROWS)
        scores = lax.dot_general(
            q_ref[mine, :], k_ref[pl.ds(0, n), :], (((1,), (1,)), ((), ())), preferred_element_type=F32
        )
        row = lax.broadcasted_iota(jnp.int32, (ROWS, n), 0) + i * ROWS
        col = lax.broadcasted_iota(jnp.int32, (ROWS, n), 1)
        scores = jnp.where(row >= col, scores * scale, -1e30)
        top = jnp.max(scores, axis=-1, keepdims=True)
        weights = jnp.exp(scores - top)
        probs = weights * (1.0 / jnp.sum(weights, axis=-1, keepdims=True))
        probs_ref[0, mine, pl.ds(0, n)] = probs
        ctx = jnp.dot(probs.astype(BF16), v_ref[pl.ds(0, n), :], preferred_element_type=F32)
        ctx = ctx.astype(BF16)
        ctx_ref[mine, :] = ctx
        even = jnp.concatenate([ctx[0:32], ctx[64:96]], axis=0)
        odd = jnp.concatenate([ctx[32:64], ctx[96:128]], axis=0)
        half = pl.ds(i * (ROWS // 2), ROWS // 2)
        keep_ref[half, :] = jnp.where(core == 0, even, odd)
        give_ref[half, :] = jnp.where(core == 0, odd, even)


def attention_forward(core, q, k, v):
    tokens, cols = q.shape
    heads = cols // HD
    head = pl.BlockSpec((tokens, HD), lambda h: (0, h))
    half = pl.BlockSpec((tokens // 2, HD), lambda h: (0, h))
    return pl.pallas_call(
        forward_kernel,
        grid=(heads,),
        in_specs=[pl.BlockSpec(memory_space=SMEM), head, head, head],
        out_specs=[head, half, half, pl.BlockSpec((1, tokens, tokens), lambda h: (h, 0, 0))],
        out_shape=[
            jax.ShapeDtypeStruct((tokens, cols), BF16),
            jax.ShapeDtypeStruct((tokens // 2, cols), BF16),
            jax.ShapeDtypeStruct((tokens // 2, cols), BF16),
            jax.ShapeDtypeStruct((heads, tokens, tokens), F32),
        ],
        compiler_params=pltpu.CompilerParams(vmem_limit_bytes=32 << 20),
        cost_estimate=pl.CostEstimate(
            flops=4 * heads * tokens * tokens * HD, bytes_accessed=4 << 20, transcendentals=heads * tokens * tokens
        ),
        name="attention_forward",
    )(core, q, k, v)


def project_kernel(at_ref, mine_ref, theirs_ref, w_ref, w2_ref, *rest):
    outs, held = rest[:-1], rest[-1]
    part = jnp.dot(mine_ref[...], w_ref[...], preferred_element_type=F32)
    part += jnp.dot(theirs_ref[...], w2_ref[...], preferred_element_type=F32)
    held[...] = part.astype(BF16)
    for i, out in enumerate(outs):
        out[...] = held[pl.ds(pl.multiple_of(at_ref[i], 32), 32), :]


def project(at, mine, theirs, w, w2, blk=1024):
    rows, cols = mine.shape
    width = w.shape[1]
    whole = pl.BlockSpec((rows, cols), lambda j: (0, 0))
    weight = pl.BlockSpec((cols, blk), lambda j: (0, j))
    chunk = pl.BlockSpec((32, blk), lambda j: (0, j))
    n = rows // 32
    return pl.pallas_call(
        project_kernel,
        grid=(width // blk,),
        in_specs=[pl.BlockSpec(memory_space=SMEM), whole, whole, weight, weight],
        out_specs=[chunk] * n,
        out_shape=[jax.ShapeDtypeStruct((32, width), BF16)] * n,
        scratch_shapes=[pltpu.VMEM((rows, blk), BF16)],
        compiler_params=pltpu.CompilerParams(vmem_limit_bytes=32 << 20),
        cost_estimate=pl.CostEstimate(
            flops=4 * rows * cols * width, bytes_accessed=11 << 20, transcendentals=0
        ),
        name="project",
    )(at, mine, theirs, w, w2)


def weight_kernel(n, at_ref, ctx_ref, w_ref, *rest):
    pieces, (wg_ref, cg_ref, held, acc) = rest[:n], rest[n:]
    for i, piece in enumerate(pieces):
        held[pl.ds(pl.multiple_of(at_ref[i], 32), 32), :] = piece[...]
    block = held[...]
    wg = lax.dot_general(ctx_ref[...], block, (((0,), (0,)), ((), ())), preferred_element_type=F32)
    wg_ref[...] = wg.astype(BF16)
    part = lax.dot_general(block, w_ref[...], (((1,), (1,)), ((), ())), preferred_element_type=F32)
    j = pl.program_id(0)

    @pl.when(j == 0)
    def _():
        acc[...] = part

    @pl.when(j > 0)
    def _():
        acc[...] += part

    @pl.when(j == pl.num_programs(0) - 1)
    def _():
        cg_ref[...] = acc[...].astype(BF16)


def weight_and_context_grads(at, ctx, w, pieces, blk=1024):
    tokens, cols = ctx.shape
    width = w.shape[1]
    n = len(pieces)
    whole = pl.BlockSpec((tokens, cols), lambda j: (0, 0))
    weight = pl.BlockSpec((cols, blk), lambda j: (0, j))
    chunk = pl.BlockSpec((32, blk), lambda j: (0, j))
    return pl.pallas_call(
        functools.partial(weight_kernel, n),
        grid=(width // blk,),
        in_specs=[pl.BlockSpec(memory_space=SMEM), whole, weight] + [chunk] * n,
        out_specs=[weight, whole],
        out_shape=[jax.ShapeDtypeStruct((cols, width), BF16), jax.ShapeDtypeStruct((tokens, cols), BF16)],
        scratch_shapes=[pltpu.VMEM((tokens, blk), BF16), pltpu.VMEM((tokens, cols), F32)],
        compiler_params=pltpu.CompilerParams(vmem_limit_bytes=32 << 20),
        cost_estimate=pl.CostEstimate(
            flops=4 * tokens * cols * width, bytes_accessed=15 << 20, transcendentals=0
        ),
        name="weight_and_context_grads",
    )(at, ctx, w, *pieces)


def backward_kernel(q_ref, k_ref, v_ref, cg_ref, probs_ref, dq_ref, dk_ref, dv_ref, dk_acc, dv_acc):
    scale = HD ** (-0.5)
    tokens = q_ref.shape[0]
    blocks = tokens // ROWS
    for i in reversed(range(blocks)):
        n = ROWS * (i + 1)
        mine, seen = pl.ds(i * ROWS, ROWS), pl.ds(0, n)
        probs = probs_ref[0, mine, seen]
        cg = cg_ref[mine, :]
        probs_grad = lax.dot_general(
            cg, v_ref[seen, :], (((1,), (1,)), ((), ())), preferred_element_type=F32
        )
        inner = jnp.sum(probs * probs_grad, axis=-1, keepdims=True)
        score_grad = (probs * (probs_grad - inner) * scale).astype(BF16)
        dq_ref[mine, :] = jnp.dot(score_grad, k_ref[seen, :], preferred_element_type=F32).astype(BF16)
        dk = lax.dot_general(score_grad, q_ref[mine, :], (((0,), (0,)), ((), ())), preferred_element_type=F32)
        dv = lax.dot_general(probs.astype(BF16), cg, (((0,), (0,)), ((), ())), preferred_element_type=F32)
        if i == blocks - 1:
            dk_acc[...] = dk
            dv_acc[...] = dv
        else:
            dk_acc[seen, :] += dk
            dv_acc[seen, :] += dv
    dk_ref[...] = dk_acc[...].astype(BF16)
    dv_ref[...] = dv_acc[...].astype(BF16)


def attention_backward(q, k, v, cg, probs):
    tokens, cols = q.shape
    heads = cols // HD
    head = pl.BlockSpec((tokens, HD), lambda h: (0, h))
    return pl.pallas_call(
        backward_kernel,
        grid=(heads,),
        in_specs=[head] * 4 + [pl.BlockSpec((1, tokens, tokens), lambda h: (h, 0, 0))],
        out_specs=[head] * 3,
        out_shape=[jax.ShapeDtypeStruct((tokens, cols), BF16)] * 3,
        scratch_shapes=[pltpu.VMEM((tokens, HD), F32)] * 2,
        compiler_params=pltpu.CompilerParams(vmem_limit_bytes=32 << 20),
        cost_estimate=pl.CostEstimate(
            flops=8 * heads * tokens * tokens * HD, bytes_accessed=4 << 20, transcendentals=0
        ),
        name="attention_backward",
    )(q, k, v, cg, probs)


def add(*terms):
    total = terms[0].astype(F32)
    for term in terms[1:]:
        total = total + term.astype(F32)
    return total.astype(BF16)


def nesterov(outer_old, moment_old, summed):
    average = summed / lax.axis_size("rep")
    pseudo_grad = outer_old - average
    new_momentum = outer_momentum * moment_old + pseudo_grad
    new_global = outer_old - outer_rate * (outer_momentum * new_momentum + pseudo_grad)
    return (new_global, new_momentum)


def outer_update(local_params, global_params, momentum, frag_index):
    chosen = frag_index[0]
    part = lax.dynamic_index_in_dim(local_params[0], chosen, 0, keepdims=False)
    outer_old = lax.dynamic_index_in_dim(global_params, chosen, 0, keepdims=False)
    moment_old = lax.dynamic_index_in_dim(momentum, chosen, 0, keepdims=False)
    for moves in REP_STEPS[:-1]:
        part = lax.reduce_precision(part.astype(F32) + send(part, moves, "rep").astype(F32), 8, 7).astype(BF16)
        part = lax.optimization_barrier(part)
    summed = part.astype(F32) + send(part, REP_STEPS[-1], "rep").astype(F32)
    return nesterov(outer_old, moment_old, summed)


def shards(
    queries, keys, values, out_weight, cotangent, local_params, global_params, momentum, frag_index
):
    q, k, v, w, x = queries[0], keys[0], values[0], out_weight[0], cotangent[0]
    me = lax.axis_index("tp")
    y, z, c = me // 4, (me // 2) % 2, me % 2
    ahead = 1 - 2 * c

    far = send(x, ACROSS)
    near = [x]
    near.append(send(x, AHEAD))
    near.append(send(x, BACK))
    near.append(send(near[1], AHEAD))
    w2 = send(w, OTHER_CORE)

    core = jnp.reshape(c, (1,)).astype(jnp.int32)
    ctx, keep, give, probs = attention_forward(core, q, k, v)
    theirs = send(give, OTHER_CORE)
    at = [
        ((jnp.mod(y + hop * ahead, N_Y)) * 2 + zz) * 32 for zz in (z, 1 - z) for hop in (0, 1, 2, 3)
    ]
    parts = project(jnp.stack(at).astype(jnp.int32), keep, theirs, w, w2)
    own, other = parts[:4], parts[4:]

    def over_y(p):
        first = send(p[2], AHEAD)
        side = send(p[3], BACK)
        second = send(add(p[1], first), AHEAD)
        return second, side

    second, side = over_y(other)
    crossed = send(add(other[0], second, side), ACROSS)

    farther = [far]
    farther.append(send(far, AHEAD))
    farther.append(send(far, BACK))
    farther.append(send(farther[1], AHEAD))

    second, side = over_y(own)
    branch_out = add(own[0], second, side, crossed)

    mine = near + farther
    pieces = mine + [send(piece, OTHER_CORE) for piece in mine]
    token_at = [
        (jnp.mod(y + hop * sign, N_Y) * 4 + zz * 2 + cc) * 32
        for cc, sign in ((c, ahead), (1 - c, -ahead))
        for zz in (z, 1 - z)
        for hop in (0, -1, 1, -2)
    ]
    weight_grad, cg = weight_and_context_grads(jnp.stack(token_at).astype(jnp.int32), ctx, w, pieces)
    dq, dk, dv = attention_backward(q, k, v, cg, probs)
    new_global, new_momentum = outer_update(local_params, global_params, momentum, frag_index)
    return (branch_out[None], weight_grad[None], dq[None], dk[None], dv[None], new_global, new_momentum)


def solution(mesh):
    placed = (
        P("rep", None, "tp"),
        P("rep", None, "tp"),
        P("rep", None, "tp"),
        P("rep", "tp", None),
        P("rep", "tp", None),
        P("rep", None, "tp", None),
        P(None, "tp", None),
        P(None, "tp", None),
        P(),
    )
    return jax.shard_map(
        shards,
        mesh=mesh,
        in_specs=placed,
        out_specs=(
            P("rep", "tp", None),
            P("rep", "tp", None),
            P("rep", None, "tp"),
            P("rep", None, "tp"),
            P("rep", None, "tp"),
            P("tp", None),
            P("tp", None),
        ),
        check_vma=False,
    )
```

```python
import functools

import jax
import jax.numpy as jnp
from jax import lax
from jax.experimental import pallas as pl
from jax.experimental.pallas import tpu as pltpu
from jax.sharding import PartitionSpec as P

HD = 128
ROWS = 256
N_Y = 4
F32 = jnp.float32
BF16 = jnp.bfloat16

outer_momentum = 0.9
outer_rate = 0.7
SMEM = pltpu.SMEM
VMEM = 24 << 20


def tp_index(y, z, c):
    return (y % N_Y) * 4 + z * 2 + c


def tp_moves(move):
    return [
        (tp_index(y, z, c), tp_index(*move(y, z, c)))
        for y in range(N_Y)
        for z in range(2)
        for c in range(2)
    ]


AHEAD = tp_moves(lambda y, z, c: (y + 1 - 2 * c, z, c))
BACK = tp_moves(lambda y, z, c: (y - 1 + 2 * c, z, c))
ACROSS = tp_moves(lambda y, z, c: (y, 1 - z, c))
OTHER_CORE = tp_moves(lambda y, z, c: (y, z, 1 - c))
REP_STEPS = [[(r, r ^ bit) for r in range(16)] for bit in (1, 2, 4, 8)]


def send(value, moves, axis="tp"):
    return lax.ppermute(value, axis, moves)


def softmax_rows(q, k, first):
    rows, seen = q.shape[0], k.shape[0]
    scores = lax.dot_general(q, k, (((1,), (1,)), ((), ())), preferred_element_type=F32)
    row = lax.broadcasted_iota(jnp.int32, (rows, seen), 0) + first
    col = lax.broadcasted_iota(jnp.int32, (rows, seen), 1)
    scores = jnp.where(row >= col, scores * HD ** (-0.5), -1e30)
    weights = jnp.exp(scores - jnp.max(scores, axis=-1, keepdims=True))
    return weights * (1.0 / jnp.sum(weights, axis=-1, keepdims=True))


def forward_kernel(core_ref, q_ref, k_ref, v_ref, ctx_ref, keep_ref, give_ref):
    core = core_ref[0]
    tokens, cols = q_ref.shape
    for h in range(cols // HD):
        head = pl.ds(h * HD, HD)
        for i in range(tokens // ROWS):
            seen, mine = pl.ds(0, ROWS * (i + 1)), pl.ds(i * ROWS, ROWS)
            probs = softmax_rows(q_ref[mine, head], k_ref[seen, head], i * ROWS)
            ctx = jnp.dot(probs.astype(BF16), v_ref[seen, head], preferred_element_type=F32).astype(BF16)
            ctx_ref[mine, head] = ctx
            even = jnp.concatenate([ctx[r : r + 32] for r in range(0, ROWS, 64)], axis=0)
            odd = jnp.concatenate([ctx[r + 32 : r + 64] for r in range(0, ROWS, 64)], axis=0)
            half = pl.ds(i * (ROWS // 2), ROWS // 2)
            keep_ref[half, head] = jnp.where(core == 0, even, odd)
            give_ref[half, head] = jnp.where(core == 0, odd, even)


def attention_forward(core, q, k, v):
    tokens, cols = q.shape
    vmem = pl.BlockSpec(memory_space=pltpu.VMEM)
    return pl.pallas_call(
        forward_kernel,
        in_specs=[pl.BlockSpec(memory_space=SMEM), vmem, vmem, vmem],
        out_specs=[vmem] * 3,
        out_shape=[
            jax.ShapeDtypeStruct((tokens, cols), BF16),
            jax.ShapeDtypeStruct((tokens // 2, cols), BF16),
            jax.ShapeDtypeStruct((tokens // 2, cols), BF16),
        ],
        compiler_params=pltpu.CompilerParams(vmem_limit_bytes=VMEM),
                name="attention_forward",
    )(core, q, k, v)


def project_kernel(at_ref, mine_ref, theirs_ref, w_ref, w2_ref, *rest):
    outs, held = rest[:-1], rest[-1]
    part = jnp.dot(mine_ref[...], w_ref[...], preferred_element_type=F32)
    part += jnp.dot(theirs_ref[...], w2_ref[...], preferred_element_type=F32)
    held[...] = part.astype(BF16)
    for i, out in enumerate(outs):
        out[...] = held[pl.ds(pl.multiple_of(at_ref[i], 32), 32), :]


def project(at, mine, theirs, w, w2, blk=3584):
    rows, cols = mine.shape
    width = w.shape[1]
    whole = pl.BlockSpec((rows, cols), lambda j: (0, 0))
    weight = pl.BlockSpec((cols, blk), lambda j: (0, j))
    chunk = pl.BlockSpec((32, blk), lambda j: (0, j))
    n = rows // 32
    return pl.pallas_call(
        project_kernel,
        grid=(width // blk,),
        in_specs=[pl.BlockSpec(memory_space=SMEM), whole, whole, weight, weight],
        out_specs=[chunk] * n,
        out_shape=[jax.ShapeDtypeStruct((32, width), BF16)] * n,
        scratch_shapes=[pltpu.VMEM((rows, blk), BF16)],
        compiler_params=pltpu.CompilerParams(vmem_limit_bytes=VMEM),
                name="project",
    )(at, mine, theirs, w, w2)


def weight_kernel(n, at_ref, ctx_ref, w_ref, *rest):
    pieces, (wg_ref, cg_ref, held, acc, flipped) = rest[:n], rest[n:]
    j = pl.program_id(0)

    @pl.when(j == 0)
    def _():
        flipped[...] = ctx_ref[...].T

    for i, piece in enumerate(pieces):
        held[pl.ds(pl.multiple_of(at_ref[i], 32), 32), :] = piece[...]
    block = held[...]
    wg = jnp.dot(flipped[...], block, preferred_element_type=F32)
    wg_ref[...] = wg.astype(BF16)
    part = lax.dot_general(block, w_ref[...], (((1,), (1,)), ((), ())), preferred_element_type=F32)

    @pl.when(j == 0)
    def _():
        acc[...] = part

    @pl.when(j > 0)
    def _():
        acc[...] += part

    @pl.when(j == pl.num_programs(0) - 1)
    def _():
        cg_ref[...] = acc[...].astype(BF16)


def weight_and_context_grads(at, ctx, w, pieces, blk=1792):
    tokens, cols = ctx.shape
    width = w.shape[1]
    n = len(pieces)
    whole = pl.BlockSpec((tokens, cols), lambda j: (0, 0))
    weight = pl.BlockSpec((cols, blk), lambda j: (0, j))
    chunk = pl.BlockSpec((32, blk), lambda j: (0, j))
    return pl.pallas_call(
        functools.partial(weight_kernel, n),
        grid=(width // blk,),
        in_specs=[pl.BlockSpec(memory_space=SMEM), whole, weight] + [chunk] * n,
        out_specs=[weight, whole],
        out_shape=[jax.ShapeDtypeStruct((cols, width), BF16), jax.ShapeDtypeStruct((tokens, cols), BF16)],
        scratch_shapes=[
            pltpu.VMEM((tokens, blk), BF16),
            pltpu.VMEM((tokens, cols), F32),
            pltpu.VMEM((cols, tokens), BF16),
        ],
        compiler_params=pltpu.CompilerParams(vmem_limit_bytes=VMEM),
                name="weight_and_context_grads",
    )(at, ctx, w, *pieces)


def backward_kernel(q_ref, k_ref, v_ref, cg_ref, dq_ref, dk_ref, dv_ref, dk_acc, dv_acc):
    tokens, cols = q_ref.shape
    blocks = tokens // ROWS
    for h in range(cols // HD):
        head = pl.ds(h * HD, HD)
        for i in reversed(range(blocks)):
            mine, seen = pl.ds(i * ROWS, ROWS), pl.ds(0, ROWS * (i + 1))
            q, k, cg = q_ref[mine, head], k_ref[seen, head], cg_ref[mine, head]
            probs = softmax_rows(q, k, i * ROWS)
            probs_grad = lax.dot_general(
                cg, v_ref[seen, head], (((1,), (1,)), ((), ())), preferred_element_type=F32
            )
            inner = jnp.sum(probs * probs_grad, axis=-1, keepdims=True)
            score_grad = (probs * (probs_grad - inner) * HD ** (-0.5)).astype(BF16)
            dq_ref[mine, head] = jnp.dot(score_grad, k, preferred_element_type=F32).astype(BF16)
            dk = lax.dot_general(score_grad, q, (((0,), (0,)), ((), ())), preferred_element_type=F32)
            dv = lax.dot_general(probs.astype(BF16), cg, (((0,), (0,)), ((), ())), preferred_element_type=F32)
            if i == blocks - 1:
                dk_acc[:, head] = dk
                dv_acc[:, head] = dv
            else:
                dk_acc[seen, head] += dk
                dv_acc[seen, head] += dv
    dk_ref[...] = dk_acc[...].astype(BF16)
    dv_ref[...] = dv_acc[...].astype(BF16)


def attention_backward(q, k, v, cg):
    tokens, cols = q.shape
    vmem = pl.BlockSpec(memory_space=pltpu.VMEM)
    return pl.pallas_call(
        backward_kernel,
        in_specs=[vmem] * 4,
        out_specs=[vmem] * 3,
        out_shape=[jax.ShapeDtypeStruct((tokens, cols), BF16)] * 3,
        scratch_shapes=[pltpu.VMEM((tokens, cols), F32)] * 2,
        compiler_params=pltpu.CompilerParams(vmem_limit_bytes=VMEM),
                name="attention_backward",
    )(q, k, v, cg)


def add(*terms):
    total = terms[0].astype(F32)
    for term in terms[1:]:
        total = total + term.astype(F32)
    return total.astype(BF16)


def nesterov(outer_old, moment_old, summed):
    average = summed / lax.axis_size("rep")
    pseudo_grad = outer_old - average
    new_momentum = outer_momentum * moment_old + pseudo_grad
    new_global = outer_old - outer_rate * (outer_momentum * new_momentum + pseudo_grad)
    return (new_global, new_momentum)


def after(value, *earlier):
    return lax.optimization_barrier((value, *earlier))[0]


class Line:
    def __init__(self):
        self.sent = []

    def send(self, value, moves):
        if len(self.sent) >= 2:
            value = after(value, self.sent[-2])
        self.sent.append(send(value, moves))
        return self.sent[-1]


def shards(
    queries, keys, values, out_weight, cotangent, local_params, global_params, momentum, frag_index
):
    q, k, v, w, x = queries[0], keys[0], values[0], out_weight[0], cotangent[0]
    q, k, v, w = (pltpu.with_memory_space_constraint(a, pltpu.HBM) for a in (q, k, v, w))
    me = lax.axis_index("tp")
    y, z, c = me // 4, (me // 2) % 2, me % 2
    ahead = 1 - 2 * c
    line = Line()

    far = send(x, ACROSS)
    near1 = line.send(x, AHEAD)
    near2 = line.send(x, BACK)
    w2 = send(w, OTHER_CORE)

    core = jnp.reshape(c, (1,)).astype(jnp.int32)
    ctx, keep, give = attention_forward(core, q, k, v)
    theirs = send(give, OTHER_CORE)
    at = [
        ((jnp.mod(y + hop * ahead, N_Y)) * 2 + zz) * 32 for zz in (z, 1 - z) for hop in (0, 1, 2, 3)
    ]
    parts = project(jnp.stack(at).astype(jnp.int32), keep, theirs, w, w2)
    own, other = parts[:4], parts[4:]
    near3 = line.send(after(near1, parts[0]), AHEAD)

    first = line.send(other[2], AHEAD)
    side = line.send(other[3], BACK)
    middle = add(other[1], first)
    second = line.send(middle, AHEAD)
    far1 = line.send(far, AHEAD)
    crossing = add(other[0], second, side)
    crossed = send(crossing, ACROSS)
    far2 = line.send(far, BACK)
    far3 = line.send(far1, AHEAD)

    first2 = line.send(own[2], AHEAD)
    side2 = line.send(own[3], BACK)
    middle2 = add(own[1], first2)
    second2 = line.send(middle2, AHEAD)
    branch_out = add(own[0], second2, side2, crossed)

    mine = [x, near1, near2, near3, far, far1, far2, far3]
    pieces = mine + [send(piece, OTHER_CORE) for piece in mine]
    token_at = [
        (jnp.mod(y + hop * sign, N_Y) * 4 + zz * 2 + cc) * 32
        for cc, sign in ((c, ahead), (1 - c, -ahead))
        for zz in (z, 1 - z)
        for hop in (0, -1, 1, -2)
    ]
    weight_grad, cg = weight_and_context_grads(jnp.stack(token_at).astype(jnp.int32), ctx, w, pieces)
    dq, dk, dv = attention_backward(q, k, v, after(cg, middle2))

    chosen = frag_index[0]
    part = lax.dynamic_index_in_dim(local_params[0], chosen, 0, keepdims=False)
    outer_old = lax.dynamic_index_in_dim(global_params, chosen, 0, keepdims=False)
    moment_old = lax.dynamic_index_in_dim(momentum, chosen, 0, keepdims=False)
    for moves, ready in zip(REP_STEPS, (near3, side, middle, far1)):
        part = after(part, ready)
        total = part.astype(F32) + send(part, moves, "rep").astype(F32)
        part = lax.reduce_precision(total, 8, 7).astype(BF16)
    new_global, new_momentum = nesterov(outer_old, moment_old, total)
    return (branch_out[None], weight_grad[None], dq[None], dk[None], dv[None], new_global, new_momentum)


def solution(mesh):
    placed = (
        P("rep", None, "tp"),
        P("rep", None, "tp"),
        P("rep", None, "tp"),
        P("rep", "tp", None),
        P("rep", "tp", None),
        P("rep", None, "tp", None),
        P(None, "tp", None),
        P(None, "tp", None),
        P(),
    )
    return jax.shard_map(
        shards,
        mesh=mesh,
        in_specs=placed,
        out_specs=(
            P("rep", "tp", None),
            P("rep", "tp", None),
            P("rep", None, "tp"),
            P("rep", None, "tp"),
            P("rep", None, "tp"),
            P("tp", None),
            P("tp", None),
        ),
        check_vma=False,
    )
```

```python
import functools

import jax
import jax.numpy as jnp
from jax import lax
from jax.experimental import pallas as pl
from jax.experimental.pallas import tpu as pltpu
from jax.sharding import PartitionSpec as P

HD = 128
ROWS = 256
N_Y = 4
F32 = jnp.float32
BF16 = jnp.bfloat16

outer_momentum = 0.9
outer_rate = 0.7
SMEM = pltpu.SMEM
VMEM = 24 << 20


def tp_index(y, z, c):
    return (y % N_Y) * 4 + z * 2 + c


def tp_moves(move):
    return [
        (tp_index(y, z, c), tp_index(*move(y, z, c)))
        for y in range(N_Y)
        for z in range(2)
        for c in range(2)
    ]


AHEAD = tp_moves(lambda y, z, c: (y + 1 - 2 * c, z, c))
BACK = tp_moves(lambda y, z, c: (y - 1 + 2 * c, z, c))
ACROSS = tp_moves(lambda y, z, c: (y, 1 - z, c))
OTHER_CORE = tp_moves(lambda y, z, c: (y, z, 1 - c))
REP_STEPS = [[(r, r ^ bit) for r in range(16)] for bit in (1, 2, 4, 8)]


def send(value, moves, axis="tp"):
    return lax.ppermute(value, axis, moves)


def softmax_rows(q, k, first):
    rows, seen = q.shape[0], k.shape[0]
    scores = lax.dot_general(q, k, (((1,), (1,)), ((), ())), preferred_element_type=F32)
    row = lax.broadcasted_iota(jnp.int32, (rows, seen), 0) + first
    col = lax.broadcasted_iota(jnp.int32, (rows, seen), 1)
    scores = jnp.where(row >= col, scores * HD ** (-0.5), -1e30)
    weights = jnp.exp(scores - jnp.max(scores, axis=-1, keepdims=True))
    return weights * (1.0 / jnp.sum(weights, axis=-1, keepdims=True))


def forward_kernel(core_ref, q_ref, k_ref, v_ref, ctx_ref, keep_ref, give_ref):
    core = core_ref[0]
    tokens, cols = q_ref.shape
    for h in range(cols // HD):
        head = pl.ds(h * HD, HD)
        for i in range(tokens // ROWS):
            seen, mine = pl.ds(0, ROWS * (i + 1)), pl.ds(i * ROWS, ROWS)
            probs = softmax_rows(q_ref[mine, head], k_ref[seen, head], i * ROWS)
            ctx = jnp.dot(probs.astype(BF16), v_ref[seen, head], preferred_element_type=F32).astype(BF16)
            ctx_ref[mine, head] = ctx
            even = jnp.concatenate([ctx[r : r + 32] for r in range(0, ROWS, 64)], axis=0)
            odd = jnp.concatenate([ctx[r + 32 : r + 64] for r in range(0, ROWS, 64)], axis=0)
            half = pl.ds(i * (ROWS // 2), ROWS // 2)
            keep_ref[half, head] = jnp.where(core == 0, even, odd)
            give_ref[half, head] = jnp.where(core == 0, odd, even)


def attention_forward(core, q, k, v):
    tokens, cols = q.shape
    vmem = pl.BlockSpec(memory_space=pltpu.VMEM)
    return pl.pallas_call(
        forward_kernel,
        in_specs=[pl.BlockSpec(memory_space=SMEM), vmem, vmem, vmem],
        out_specs=[vmem] * 3,
        out_shape=[
            jax.ShapeDtypeStruct((tokens, cols), BF16),
            jax.ShapeDtypeStruct((tokens // 2, cols), BF16),
            jax.ShapeDtypeStruct((tokens // 2, cols), BF16),
        ],
        compiler_params=pltpu.CompilerParams(vmem_limit_bytes=VMEM),
                name="attention_forward",
    )(core, q, k, v)


def project_kernel(at_ref, mine_ref, theirs_ref, w_ref, w2_ref, *rest):
    outs, held = rest[:-1], rest[-1]
    part = jnp.dot(mine_ref[...], w_ref[...], preferred_element_type=F32)
    part += jnp.dot(theirs_ref[...], w2_ref[...], preferred_element_type=F32)
    held[...] = part.astype(BF16)
    for i, out in enumerate(outs):
        out[...] = held[pl.ds(pl.multiple_of(at_ref[i], 32), 32), :]


def project(at, mine, theirs, w, w2, blk=3584):
    rows, cols = mine.shape
    width = w.shape[1]
    whole = pl.BlockSpec((rows, cols), lambda j: (0, 0))
    weight = pl.BlockSpec((cols, blk), lambda j: (0, j))
    chunk = pl.BlockSpec((32, blk), lambda j: (0, j))
    n = rows // 32
    return pl.pallas_call(
        project_kernel,
        grid=(width // blk,),
        in_specs=[pl.BlockSpec(memory_space=SMEM), whole, whole, weight, weight],
        out_specs=[chunk] * n,
        out_shape=[jax.ShapeDtypeStruct((32, width), BF16)] * n,
        scratch_shapes=[pltpu.VMEM((rows, blk), BF16)],
        compiler_params=pltpu.CompilerParams(vmem_limit_bytes=VMEM),
                name="project",
    )(at, mine, theirs, w, w2)


def weight_kernel(n, at_ref, ctx_ref, w_ref, *rest):
    pieces, (wg_ref, cg_ref, held, acc, flipped) = rest[:n], rest[n:]
    j = pl.program_id(0)

    @pl.when(j == 0)
    def _():
        flipped[...] = ctx_ref[...].T

    for i, piece in enumerate(pieces):
        held[pl.ds(pl.multiple_of(at_ref[i], 32), 32), :] = piece[...]
    block = held[...]
    wg = jnp.dot(flipped[...], block, preferred_element_type=F32)
    wg_ref[...] = wg.astype(BF16)
    part = lax.dot_general(block, w_ref[...], (((1,), (1,)), ((), ())), preferred_element_type=F32)

    @pl.when(j == 0)
    def _():
        acc[...] = part

    @pl.when(j > 0)
    def _():
        acc[...] += part

    @pl.when(j == pl.num_programs(0) - 1)
    def _():
        cg_ref[...] = acc[...].astype(BF16)


def weight_and_context_grads(at, ctx, w, pieces, blk=1792):
    tokens, cols = ctx.shape
    width = w.shape[1]
    n = len(pieces)
    whole = pl.BlockSpec((tokens, cols), lambda j: (0, 0))
    weight = pl.BlockSpec((cols, blk), lambda j: (0, j))
    chunk = pl.BlockSpec((32, blk), lambda j: (0, j))
    return pl.pallas_call(
        functools.partial(weight_kernel, n),
        grid=(width // blk,),
        in_specs=[pl.BlockSpec(memory_space=SMEM), whole, weight] + [chunk] * n,
        out_specs=[weight, whole],
        out_shape=[jax.ShapeDtypeStruct((cols, width), BF16), jax.ShapeDtypeStruct((tokens, cols), BF16)],
        scratch_shapes=[
            pltpu.VMEM((tokens, blk), BF16),
            pltpu.VMEM((tokens, cols), F32),
            pltpu.VMEM((cols, tokens), BF16),
        ],
        compiler_params=pltpu.CompilerParams(vmem_limit_bytes=VMEM),
                name="weight_and_context_grads",
    )(at, ctx, w, *pieces)


def backward_kernel(q_ref, k_ref, v_ref, cg_ref, dq_ref, dk_ref, dv_ref, dk_acc, dv_acc):
    tokens, cols = q_ref.shape
    blocks = tokens // ROWS
    for h in range(cols // HD):
        head = pl.ds(h * HD, HD)
        for i in reversed(range(blocks)):
            mine, seen = pl.ds(i * ROWS, ROWS), pl.ds(0, ROWS * (i + 1))
            q, k, cg = q_ref[mine, head], k_ref[seen, head], cg_ref[mine, head]
            probs = softmax_rows(q, k, i * ROWS)
            probs_grad = lax.dot_general(
                cg, v_ref[seen, head], (((1,), (1,)), ((), ())), preferred_element_type=F32
            )
            inner = jnp.sum(probs * probs_grad, axis=-1, keepdims=True)
            score_grad = (probs * (probs_grad - inner) * HD ** (-0.5)).astype(BF16)
            dq_ref[mine, head] = jnp.dot(score_grad, k, preferred_element_type=F32).astype(BF16)
            dk = lax.dot_general(score_grad, q, (((0,), (0,)), ((), ())), preferred_element_type=F32)
            dv = lax.dot_general(probs.astype(BF16), cg, (((0,), (0,)), ((), ())), preferred_element_type=F32)
            if i == blocks - 1:
                dk_acc[:, head] = dk
                dv_acc[:, head] = dv
            else:
                dk_acc[seen, head] += dk
                dv_acc[seen, head] += dv
    dk_ref[...] = dk_acc[...].astype(BF16)
    dv_ref[...] = dv_acc[...].astype(BF16)


def attention_backward(q, k, v, cg):
    tokens, cols = q.shape
    vmem = pl.BlockSpec(memory_space=pltpu.VMEM)
    return pl.pallas_call(
        backward_kernel,
        in_specs=[vmem] * 4,
        out_specs=[vmem] * 3,
        out_shape=[jax.ShapeDtypeStruct((tokens, cols), BF16)] * 3,
        scratch_shapes=[pltpu.VMEM((tokens, cols), F32)] * 2,
        compiler_params=pltpu.CompilerParams(vmem_limit_bytes=VMEM),
                name="attention_backward",
    )(q, k, v, cg)


def add(*terms):
    total = terms[0].astype(F32)
    for term in terms[1:]:
        total = total + term.astype(F32)
    return total.astype(BF16)


def nesterov(outer_old, moment_old, summed):
    average = summed / lax.axis_size("rep")
    pseudo_grad = outer_old - average
    new_momentum = outer_momentum * moment_old + pseudo_grad
    new_global = outer_old - outer_rate * (outer_momentum * new_momentum + pseudo_grad)
    return (new_global, new_momentum)


def after(value, *earlier):
    return lax.optimization_barrier((value, *earlier))[0]


class Line:
    def __init__(self):
        self.sent = []

    def send(self, value, moves):
        if len(self.sent) >= 2:
            value = after(value, self.sent[-2])
        self.sent.append(send(value, moves))
        return self.sent[-1]


def shards(
    queries, keys, values, out_weight, cotangent, local_params, global_params, momentum, frag_index
):
    q, k, v, w, x = queries[0], keys[0], values[0], out_weight[0], cotangent[0]
    q, k, v, w = (pltpu.with_memory_space_constraint(a, pltpu.HBM) for a in (q, k, v, w))
    me = lax.axis_index("tp")
    y, z, c = me // 4, (me // 2) % 2, me % 2
    ahead = 1 - 2 * c
    line = Line()

    far = send(x, ACROSS)
    near1 = line.send(x, AHEAD)
    near2 = line.send(x, BACK)
    w2 = send(w, OTHER_CORE)

    core = jnp.reshape(c, (1,)).astype(jnp.int32)
    ctx, keep, give = attention_forward(core, q, k, v)
    theirs = send(give, OTHER_CORE)
    at = [
        ((jnp.mod(y + hop * ahead, N_Y)) * 2 + zz) * 32 for zz in (z, 1 - z) for hop in (0, 1, 2, 3)
    ]
    parts = project(jnp.stack(at).astype(jnp.int32), keep, theirs, w, w2)
    own, other = parts[:4], parts[4:]
    near3 = line.send(after(near1, parts[0]), AHEAD)

    first = line.send(other[2], AHEAD)
    side = line.send(other[3], BACK)
    middle = add(other[1], first)
    second = line.send(middle, AHEAD)
    far1 = line.send(far, AHEAD)
    crossing = add(other[0], second, side)
    crossed = send(crossing, ACROSS)
    far2 = line.send(far, BACK)
    far3 = line.send(far1, AHEAD)

    first2 = line.send(own[2], AHEAD)
    side2 = line.send(own[3], BACK)
    middle2 = add(own[1], first2)
    second2 = line.send(middle2, AHEAD)
    branch_out = add(own[0], second2, side2, crossed)

    mine = [x, near1, near2, near3, far, far1, far2, far3]
    pieces = mine + [send(piece, OTHER_CORE) for piece in mine]
    token_at = [
        (jnp.mod(y + hop * sign, N_Y) * 4 + zz * 2 + cc) * 32
        for cc, sign in ((c, ahead), (1 - c, -ahead))
        for zz in (z, 1 - z)
        for hop in (0, -1, 1, -2)
    ]
    weight_grad, cg = weight_and_context_grads(jnp.stack(token_at).astype(jnp.int32), ctx, w, pieces)
    dq, dk, dv = attention_backward(q, k, v, after(cg, middle2))

    chosen = frag_index[0]
    part = lax.dynamic_index_in_dim(local_params[0], chosen, 0, keepdims=False)
    outer_old = lax.dynamic_index_in_dim(global_params, chosen, 0, keepdims=False)
    moment_old = lax.dynamic_index_in_dim(momentum, chosen, 0, keepdims=False)
    for moves, ready in zip(REP_STEPS, (near3, side, second, far1)):
        part = after(part, ready)
        total = part.astype(F32) + send(part, moves, "rep").astype(F32)
        part = lax.reduce_precision(total, 8, 7).astype(BF16)
    new_global, new_momentum = nesterov(outer_old, moment_old, total)
    return (branch_out[None], weight_grad[None], dq[None], dk[None], dv[None], new_global, new_momentum)


def solution(mesh):
    placed = (
        P("rep", None, "tp"),
        P("rep", None, "tp"),
        P("rep", None, "tp"),
        P("rep", "tp", None),
        P("rep", "tp", None),
        P("rep", None, "tp", None),
        P(None, "tp", None),
        P(None, "tp", None),
        P(),
    )
    return jax.shard_map(
        shards,
        mesh=mesh,
        in_specs=placed,
        out_specs=(
            P("rep", "tp", None),
            P("rep", "tp", None),
            P("rep", None, "tp"),
            P("rep", None, "tp"),
            P("rep", None, "tp"),
            P("tp", None),
            P("tp", None),
        ),
        check_vma=False,
    )
```
